32 devices in a mesh: pairs: 8 (over z, x), grp: 4 (over y, core).
Axes of the slice: x: 2, y: 2, z: 4, core: 2. Of those that a mesh axis runs over, the one named last changes fastest.
Arguments:
- coefficients: bfloat16 [128, 512, 128], P('pairs', 'grp'), may hold values from -0.4140625 to 0.4140625
- domain: int32 [128, 512], P('pairs', 'grp'), may hold values from 0 to 767, as said below
- coupling_owner: int32 [128, 8], P('pairs'), may hold values from 0 to 7, all different within a row; in each aligned block of 16 rows (0 to 15, 16 to 31, ...) at most 16 rows name the same one
- coupling_slot: int32 [128, 8], P('pairs'), may hold values from 0 to 15
- coupling_fock: float32 [128, 8], P('pairs'), may hold values from -0.5 to 0.5
- exchange_integrals: float32 [128, 128, 128], P('pairs'), may hold values from -6 to 6
- pno_energy: float32 [128, 128], P('pairs'), may hold values from 0.3 to 3
- pair_shift: float32 [128], P('pairs'), may hold values from 0.4 to 2
- amplitudes_start: float32 [128, 128, 128], P('pairs'), may hold values from -1.8 to 1.8
Outputs:
- amplitudes: float32 [128, 128, 128], P('pairs')
The draws below stay inside these ranges and needn't reach their ends.
Inputs may be any that keep to these rules, and one draw needn't show every extreme that they name: `coupling_owner`: each row names different indices. Among the 16 rows of one index of pairs no value is named more than 16 times, a bound that some block reaches. `domain`: for each pair and each g from 0 to 3, the entries g * 128 to (g + 1) * 128 - 1 are distinct numbers from g * 192 to (g + 1) * 192 - 1.
All inputs are finite; a program needn't handle non-finite values.
Results may differ from the reference program's by a relative error of at most 0.0025.
Values may be sent and summed in bfloat16 or wider, within the bound.
A program may use at most 128 MiB of HBM per device.

```python
import math
import jax
import jax.numpy as jnp
import numpy as np
from jax import lax

NPNO = 128
DOM = 512
NB = 192
NCPL = 8
ITERS = 2
PAIRS_DEV = 16
NPAIRS = 128
DOMB = 128
MOST = 16
N_PAIRS = 8


def draw_domain(key, part):
    block_count = DOM // DOMB
    pair_keys = jax.random.split(key, NPAIRS * block_count)
    chosen = jax.vmap(lambda item_key: jax.random.permutation(item_key, NB)[:DOMB])(pair_keys)
    chosen = chosen.reshape(NPAIRS, block_count, DOMB).astype(jnp.int32)
    offsets = (jnp.arange(block_count, dtype=jnp.int32) * NB)[None, :, None]
    return (chosen + offsets).reshape(NPAIRS, DOM).astype(jnp.int32)


def touch_ends(entries, key, least, high):
    index_at = [jax.random.randint(jax.random.fold_in(key, axis), (), 0, length) for axis, length in enumerate(entries.shape)]
    longest = entries.shape.index(max(entries.shape))
    next_to = index_at[:longest] + [(index_at[longest] + 1) % entries.shape[longest]] + index_at[longest + 1:]
    return entries.at[tuple(index_at)].set(least).at[tuple(next_to)].set(high)


def steps_of(own_key, extent, pieces, smallest, high):
    level, own = 1.0, jax.random.fold_in(own_key, 6)
    for axis_at, blocks in pieces:
        steps = jnp.exp(jax.random.uniform(jax.random.fold_in(own, axis_at), (blocks,), jnp.float32, smallest / len(pieces), high / len(pieces)))
        level = level * jnp.repeat(steps, extent[axis_at] // blocks).reshape([-1 if axis == axis_at else 1 for axis in range(len(extent))])
    return level


def shared_out(rng, own, number, rows, amount, top, limit, skew):
    order = jax.random.permutation(rng, amount)
    packed, ordinary = shares(amount, rows * top, limit, skew, True), shares(amount, rows * top, limit, skew, False)
    places = jnp.arange(amount)

    def named(tallies, turn):
        used = int((tallies > 0).sum())
        fixed = max(1, used // 4)
        shifted = fixed + (places - fixed + turn * (used - fixed)) % max(1, amount - fixed)
        return jnp.zeros((amount,), jnp.int32).at[order[jnp.where(places < fixed, places, shifted)]].set(jnp.asarray(tallies, jnp.int32))

    tallies = jnp.where(number % 4 == 0, named(packed, number // 4), named(ordinary, number - number // 4 - 1))
    mixed = jax.random.permutation(jax.random.fold_in(own, 3), amount)
    donor, taker = mixed[0:amount // 2 * 2:2], mixed[1:amount // 2 * 2:2]
    room = jnp.minimum(tallies[donor] - 1, limit - tallies[taker]) // 2
    room = jnp.where((donor == order[0]) | (taker == order[0]) | (tallies[taker] == 0), 0, jnp.maximum(room, 0))
    shifted = jax.random.randint(jax.random.fold_in(own, 4), (amount // 2,), 0, 1 << 20) % (room + 1)
    tallies = tallies.at[donor].add(-shifted).at[taker].add(shifted)
    labels = jnp.searchsorted(jnp.cumsum(tallies), jnp.arange(rows * top), side="right").astype(jnp.int32)
    table = labels.reshape(top, rows).T
    table = table[jax.random.permutation(jax.random.fold_in(own, 1), rows)]
    turn = jax.random.randint(jax.random.fold_in(own, 2), (rows, 1), 0, top)
    return jnp.take_along_axis(table, (jnp.arange(top)[None, :] + turn) % top, axis=1)


def shares(count, total, reach, skew, full):
    weights = [(1 << 20) // math.isqrt(standing ** skew) + 1 for standing in range(1, count + 1)]
    largest = reach if full else min(reach, max(-(-total // count), total * weights[0] // sum(weights)))
    least = 1 if total - largest >= count - 1 else 0
    holding, spare = [largest] + [least] * (count - 1), total - largest - least * (count - 1)
    while spare > 0:
        candidates = [i for i in range(1, count) if holding[i] < largest] or [i for i in range(1, count) if holding[i] < reach]
        mass, budget = sum([weights[i] for i in candidates]), spare
        for i in candidates:
            more = min(reach - holding[i], max(1, budget * weights[i] // mass), spare)
            holding[i] = holding[i] + more
            spare = spare - more
    return np.array(holding)


def gaussian(own_key, dims, spread, reach, pieces=(), kind=jnp.bfloat16):
    loudness = steps_of(own_key, dims, pieces, -0.22, 0.18) if pieces else 1.0
    drawn = jax.random.normal(own_key, dims, jnp.float32) * spread * loudness
    return jnp.minimum(jnp.maximum(drawn, -reach), reach).astype(kind)


def setup_inputs(seed: int = 0) -> dict:
    seeds = jax.random.split(jax.random.key(seed), 10)
    coefficients = gaussian(seeds[0], (NPAIRS, DOM, NPNO), ((NPNO * DOM * DOMB / NB) ** -0.25), 0.4140625, ((0, 8), (1, 4)))
    domain = draw_domain(jax.random.fold_in(seeds[9], 71), 0)
    coupling_owner_keys = jax.random.split(jax.random.fold_in(seeds[2], 1), NPAIRS // PAIRS_DEV)
    coupling_owner_turns = jax.random.permutation(jax.random.fold_in(seeds[2], 3), NPAIRS // PAIRS_DEV)
    coupling_owner = jax.vmap(lambda own, number: shared_out(jax.random.fold_in(seeds[2], 2), own, number, PAIRS_DEV, N_PAIRS, NCPL, MOST, 2))(coupling_owner_keys, coupling_owner_turns).reshape((NPAIRS, NCPL))
    coupling_slot = touch_ends(jax.random.randint(seeds[3], (NPAIRS, NCPL), 0, PAIRS_DEV), jax.random.fold_in(seeds[3], 1), 0, PAIRS_DEV - 1).astype(jnp.int32)
    coupling_fock = jnp.clip(jax.random.uniform(seeds[4], (NPAIRS, NCPL), jnp.float32, -0.5, 0.5) * steps_of(seeds[4], (NPAIRS, NCPL), ((0, 8),), -0.4, 0.0), -0.5, 0.5)
    exchange_integrals = gaussian(seeds[5], (NPAIRS, NPNO, NPNO), 1.0, 6.0, ((0, 8),), jnp.float32)
    pno_energy = jnp.clip(jnp.exp(math.log(3.0) - 2.3025851 * jax.random.uniform(seeds[6], (NPAIRS, NPNO), jnp.float32) ** steps_of(seeds[6], (NPAIRS, NPNO), ((0, 8),), -0.2, 0.2)), 0.3, 3.0)
    pair_shift = jnp.clip(jnp.exp(math.log(2.0) - 1.609438 * jax.random.uniform(seeds[7], (NPAIRS,), jnp.float32) ** steps_of(seeds[7], (NPAIRS,), ((0, 8),), -0.2, 0.2)), 0.4, 2.0)
    amplitudes_start = gaussian(seeds[8], (NPAIRS, NPNO, NPNO), 0.3, 1.8, ((0, 8),), jnp.float32)
    return {"coefficients": coefficients, "domain": domain, "coupling_owner": coupling_owner, "coupling_slot": coupling_slot, "coupling_fock": coupling_fock, "exchange_integrals": exchange_integrals, "pno_energy": pno_energy, "pair_shift": pair_shift, "amplitudes_start": amplitudes_start}


def reference(coefficients, domain, coupling_owner, coupling_slot, coupling_fock, exchange_integrals, pno_energy, pair_shift, amplitudes_start):
    pair_count = coefficients.shape[0]
    total_functions = NB * (DOM // DOMB)
    source = (PAIRS_DEV * coupling_owner + coupling_slot).astype(jnp.int32)
    wide = coefficients.astype(jnp.float32)
    expanded = jnp.zeros((pair_count, total_functions, NPNO), jnp.float32)
    expanded = expanded.at[jnp.arange(pair_count, dtype=jnp.int32)[:, None], domain].set(wide)

    def intersection_one(operand):
        coef_target, dom_target, src = operand
        picked_rows = expanded[src][:, dom_target, :]
        product = jnp.einsum("ra,krc->kac", coef_target, picked_rows, precision=lax.Precision.HIGHEST)
        return product.astype(jnp.bfloat16)

    intersection = lax.map(intersection_one, (wide, domain, source))
    denominator = pno_energy[:, :, None] + pno_energy[:, None, :] + pair_shift[:, None, None]
    amplitudes = amplitudes_start
    for iteration in range(ITERS):
        sendable = amplitudes.astype(jnp.bfloat16)

        def couple(operand):
            intersection_target, src, fock_target = operand
            source_amp = sendable[src].astype(jnp.float32)
            intersection_wide = intersection_target.astype(jnp.float32)
            half_proj = jnp.einsum("kac,kcd->kad", intersection_wide, source_amp, precision=lax.Precision.HIGHEST)
            half_proj = lax.optimization_barrier(half_proj.astype(jnp.bfloat16)).astype(jnp.float32)
            projected = jnp.einsum("kad,kbd->kab", half_proj, intersection_wide, precision=lax.Precision.HIGHEST)
            return jnp.sum(fock_target[:, None, None] * projected, axis=0)

        coupled = lax.map(couple, (intersection, source, coupling_fock))
        amplitudes = -(exchange_integrals + coupled) / denominator
    return amplitudes
```

```python
import functools

import jax
import jax.numpy as jnp
from jax import lax
from jax.experimental import pallas as pl
from jax.experimental.pallas import tpu as pltpu
from jax.sharding import PartitionSpec as P

NB = 192
MESH = pl.DeviceIdType.MESH
F32, BF16 = jnp.float32, jnp.bfloat16


def ring_position(rank, n):
    odd = rank % 2
    return (1 - odd) * (rank // 2) + odd * (n - 1 - rank // 2)


def ring_rank(position, n):
    back = position // (n // 2)
    return (1 - back) * 2 * position + back * (2 * (n - 1 - position) + 1)


def places(n):
    p, g = lax.axis_index("pairs"), lax.axis_index("grp")
    position = ring_position(p, n)
    core, half = g % 2, g // 2
    mate = 2 * half + (1 - core)
    across = 2 * (1 - half) + core
    return p, g, position, mate, across


def at(position, n):
    return ring_rank((position + n) % n, n)


def greet(peers):
    barrier = pltpu.get_barrier_semaphore()
    for peer in peers:
        pl.semaphore_signal(barrier, inc=1, device_id=peer, device_id_type=MESH)
    pl.semaphore_wait(barrier, len(peers))


def remote(src, dst, send, recv, peer):
    return pltpu.make_async_remote_copy(
        src_ref=src, dst_ref=dst, send_sem=send, recv_sem=recv, device_id=peer, device_id_type=MESH
    )


def ring_parts(steps, parts):
    def of(step, direction):
        if step < steps:
            return tuple(range(parts))
        return tuple(c for c in range(parts) if c % 2 == direction)

    return of


def intersections(
    n, slot_ref, c_ref, dom_ref, out_ref,
    cbuf, dbuf, turned, wide, own, msend, mrecv, ysend, yrecv, keep,
    rs, rr, ms, mr, ys, yr,
):
    p, g, position, mate, across = places(n)
    pc = c_ref.shape[0]
    quarter = pc // 4
    rows = c_ref.shape[1]
    steps = n // 2
    right, left = at(position + 1, n), at(position - 1, n)
    ring_peer = (lambda r: (r, g))
    peers = [(right, g), (left, g), (p, mate), (p, across)]
    greet(peers)
    parts_of = ring_parts(steps, 3)
    hp = pc // 2

    def part(ref_c, ref_d, c):
        if c == 2:
            return ref_d
        return ref_c.at[pl.ds(c * hp, hp)]

    def move(step, direction, c):
        offset = -(step - 1) if direction == 0 else step - 1
        rank = at(position + offset, n)
        if step == 1:
            src = part(c_ref, dom_ref, c)
        else:
            src = part(cbuf.at[rank], dbuf.at[rank], c)
        dst = part(cbuf.at[rank], dbuf.at[rank], c)
        return remote(
            src, dst, rs.at[direction, step - 1, c], rr.at[direction, step - 1, c],
            ring_peer(right if direction == 0 else left),
        )

    def arrive(step, direction, c):
        offset = -step if direction == 0 else step
        rank = at(position + offset, n)
        dst = part(cbuf.at[rank], dbuf.at[rank], c)
        remote(
            dst, dst, rs.at[direction, step - 1, c], rr.at[direction, step - 1, c],
            ring_peer(left if direction == 0 else right),
        ).wait_recv()

    for c in (2, 0, 1):
        for d in (0, 1):
            if c in parts_of(1, d):
                move(1, d, c).start()

    base = g * NB
    lines = lax.broadcasted_iota(jnp.int32, (NB, rows), 0)
    core, half = g % 2, g // 2

    def expand(block, doms):
        def one(s, carry):
            hit = (lines == (doms[pl.ds(s, 1), :] - base)).astype(F32).astype(BF16)
            wide[s] = jnp.dot(hit, block[s], preferred_element_type=F32).astype(BF16)
            return carry

        lax.fori_loop(0, pc, one, 0, unroll=8)

    def mate_copy(k, rank):
        return remote(msend.at[k % 2], mrecv.at[rank], ms.at[k], mr.at[k], (p, mate))

    def across_copy(k, rank):
        return remote(ysend.at[k % 2], yrecv.at[rank], ys.at[k], yr.at[k], (p, across))

    ranks = []

    def product(t, rank):
        return jnp.dot(turned[t], wide[slot_ref[t, rank]], preferred_element_type=F32)

    def links(k, rank):
        if k >= 2:
            mate_copy(k - 2, ranks[k - 2]).wait_send()

        def theirs(i, carry):
            t = (2 * (i // quarter) + 1 - core) * quarter + i % quarter
            msend[k % 2, i] = product(t, rank)
            return carry

        lax.fori_loop(0, 2 * quarter, theirs, 0, unroll=8)
        mate_copy(k, rank).start()

        def ours(i, carry):
            t = (2 * (i // quarter) + core) * quarter + i % quarter
            own[k % 2, i] = product(t, rank)
            return carry

        lax.fori_loop(0, 2 * quarter, ours, 0, unroll=8)

    def finish(k):
        rank = ranks[k]
        if k >= 2:
            across_copy(k - 2, ranks[k - 2]).wait_send()
        mate_copy(k, rank).wait_recv()

        def send(j, carry):
            i = (1 - half) * quarter + j
            ysend[k % 2, j] = own[k % 2, i] + mrecv[rank, i]
            return carry

        lax.fori_loop(0, quarter, send, 0)
        across_copy(k, rank).start()

        def hold(j, carry):
            i = half * quarter + j
            keep[rank, j] = own[k % 2, i] + mrecv[rank, i]
            return carry

        lax.fori_loop(0, quarter, hold, 0)

    def process(rank):
        k = len(ranks)
        ranks.append(rank)
        links(k, rank)
        if k >= 1:
            finish(k - 1)

    expand(c_ref, dom_ref)

    def turn(t, carry):
        turned[t] = wide[t].astype(F32).T.astype(BF16)
        return carry

    lax.fori_loop(0, pc, turn, 0, unroll=2)
    process(p)
    for step in range(1, steps + 1):
        for c in (2, 0, 1):
            for d in (0, 1):
                if c in parts_of(step, d):
                    arrive(step, d, c)
                if step < steps and c in parts_of(step + 1, d):
                    move(step + 1, d, c).start()
        for d in (0, 1) if step < steps else (0,):
            rank = at(position + (-step if d == 0 else step), n)
            expand(cbuf.at[rank], dbuf.at[rank])
            process(rank)
    finish(n - 1)
    for k in range(n):
        rank = ranks[k]
        across_copy(k, rank).wait_recv()

        def last(j, carry):
            out_ref[rank, j] = (keep[rank, j] + yrecv[rank, j]).astype(BF16)
            return carry

        lax.fori_loop(0, quarter, last, 0)
    for k in (n - 2, n - 1):
        mate_copy(k, ranks[k]).wait_send()
        across_copy(k, ranks[k]).wait_send()
    for step in range(1, steps + 1):
        for d in (0, 1):
            for c in parts_of(step, d):
                move(step, d, c).wait_send()


def iteration(
    n, first, slot_ref, fock_ref, shift_ref, start_ref, x_ref, k_ref, e_ref, out_ref,
    abuf, stage, acc, mine, theirs, rs, rr, ms, mr, ys, yr, fs, fr,
):
    p, g, position, mate, across = places(n)
    pc = k_ref.shape[0]
    width = k_ref.shape[1]
    quarter = pc // 4
    steps = n // 2
    right, left = at(position + 1, n), at(position - 1, n)
    peers = [(right, g), (left, g), (p, mate), (p, across)]
    diagonal = 3 - g
    if not first:
        peers.append((p, diagonal))
    greet(peers)
    parts_of = ring_parts(steps, 2)

    def span(rank, c):
        group = g if c == 0 else across
        return abuf.at[pl.ds(rank * pc + group * quarter, quarter)]

    def move(step, direction, c):
        offset = -(step - 1) if direction == 0 else step - 1
        ref = span(at(position + offset, n), c)
        src = start_ref if (step == 1 and c == 0 and not first) else ref
        return remote(
            src, ref, rs.at[direction, step - 1, c], rr.at[direction, step - 1, c],
            (right if direction == 0 else left, g),
        )

    def arrive(step, direction, c):
        offset = -step if direction == 0 else step
        ref = span(at(position + offset, n), c)
        remote(
            ref, ref, rs.at[direction, step - 1, c], rr.at[direction, step - 1, c],
            (left if direction == 0 else right, g),
        ).wait_recv()

    def mate_copy(k, rank, c, src=None):
        ref = span(rank, c)
        return remote(ref if src is None else src, ref, ms.at[k, c], mr.at[k, c], (p, mate))

    def mate_wait(k, rank, c):
        group = mate if c == 0 else 3 - g
        ref = abuf.at[pl.ds(rank * pc + group * quarter, quarter)]
        remote(ref, ref, ms.at[k, c], mr.at[k, c], (p, mate)).wait_recv()

    if first:
        def copy_own(i, carry):
            abuf[p * pc + i] = start_ref[i].astype(BF16)
            return carry

        for c in (0, 1):
            group = g if c == 0 else across
            lax.fori_loop(group * quarter, (group + 1) * quarter, copy_own, 0)
            for d in (0, 1):
                if c in parts_of(1, d):
                    move(1, d, c).start()
        for group in (mate, 3 - g):
            lax.fori_loop(group * quarter, (group + 1) * quarter, copy_own, 0)
    else:
        ycopy = remote(
            start_ref, span(p, 0), ys, yr, (p, across)
        )
        ycopy.start()
        for d in (0, 1):
            move(1, d, 0).start()
        mate_copy(0, p, 0, start_ref).start()

        def copy_own(i, carry):
            abuf[p * pc + g * quarter + i] = start_ref[i]
            return carry

        lax.fori_loop(0, quarter, copy_own, 0)
        ref = span(p, 1)
        remote(ref, ref, ys, yr, (p, across)).wait_recv()
        for d in (0, 1):
            move(1, d, 1).start()
        mate_copy(0, p, 1).start()
        mate_wait(0, p, 0)
        mate_wait(0, p, 1)

    acc[...] = jnp.zeros_like(acc)

    def couple(rank):
        def copy(i, carry):
            stage[i] = abuf[rank * pc + i]
            return carry

        lax.fori_loop(0, pc, copy, 0, unroll=4)

        def one(j, carry):
            t = g * quarter + j
            source = stage[slot_ref[t, rank]]
            x = x_ref[rank, j]
            h = jnp.dot(x, source, preferred_element_type=F32).astype(BF16)
            y = lax.dot_general(h, x, (((1,), (1,)), ((), ())), preferred_element_type=F32)
            acc[j] += fock_ref[t, rank] * y
            return carry

        lax.fori_loop(0, quarter, one, 0, unroll=4)

    couple(p)
    pending = []
    k = 0
    for step in range(1, steps + 1):
        for c in (0, 1):
            for d in (0, 1):
                rank = at(position + (-step if d == 0 else step), n)
                if c in parts_of(step, d):
                    arrive(step, d, c)
                    if step < steps and c in parts_of(step + 1, d):
                        move(step + 1, d, c).start()
                    kk = 2 * step - 1 + (d if step < steps else 0)
                    mate_copy(kk, rank, c).start()
        for kk, rank in pending:
            for c in (0, 1):
                mate_wait(kk, rank, c)
            couple(rank)
        pending = []
        for d in (0, 1) if step < steps else (0,):
            pending.append((2 * step - 1 + d, at(position + (-step if d == 0 else step), n)))
    for kk, rank in pending:
        for c in (0, 1):
            mate_wait(kk, rank, c)
        couple(rank)

    def scaled(t, total):
        row = jnp.broadcast_to(e_ref[pl.ds(t, 1), :], (width, width))
        return -(k_ref[t] + total) / (row.T + row + shift_ref[t, 0])

    if first:
        def result(j, carry):
            out_ref[j] = scaled(g * quarter + j, acc[j]).astype(BF16)
            return carry

        lax.fori_loop(0, quarter, result, 0)
    else:
        def pack(j, carry):
            mine[j] = acc[j]
            return carry

        lax.fori_loop(0, quarter, pack, 0)
        others = (across, diagonal, mate)
        for i, other in enumerate(others):
            remote(mine, theirs.at[i], fs.at[i], fr.at[i], (p, other)).start()

        def result(j, carry):
            t = g * quarter + j
            out_ref[t] = scaled(t, acc[j])
            return carry

        lax.fori_loop(0, quarter, result, 0)
        for i in (2, 0, 1):
            other = others[i]
            copy = remote(mine, theirs.at[i], fs.at[i], fr.at[i], (p, other))
            copy.wait_recv()

            def rest(j, carry):
                t = other * quarter + j
                out_ref[t] = scaled(t, theirs[i, j])
                return carry

            lax.fori_loop(0, quarter, rest, 0)
        for i, other in enumerate(others):
            remote(mine, theirs.at[i], fs.at[i], fr.at[i], (p, other)).wait_send()
        remote(start_ref, span(p, 0), ys, yr, (p, across)).wait_send()
        mate_copy(0, p, 0, start_ref).wait_send()
        mate_copy(0, p, 1).wait_send()
    for kk in range(1, n):
        for c in (0, 1):
            mate_copy(kk, p, c).wait_send()
    for step in range(1, steps + 1):
        for d in (0, 1):
            for c in parts_of(step, d):
                move(step, d, c).wait_send()


def on_device(
    coefficients, domain, coupling_owner, coupling_slot, coupling_fock,
    exchange_integrals, pno_energy, pair_shift, amplitudes_start,
):
    n = lax.axis_size("pairs")
    pc, rows, width = coefficients.shape
    quarter = pc // lax.axis_size("grp")
    steps = n // 2
    named = coupling_owner[:, :, None] == jnp.arange(n, dtype=jnp.int32)[None, None, :]
    slots = jnp.sum(jnp.where(named, coupling_slot[:, :, None], 0), axis=1)
    focks = jnp.sum(jnp.where(named, coupling_fock[:, :, None], 0.0), axis=1)
    vmem, smem = pl.BlockSpec(memory_space=pltpu.VMEM), pl.BlockSpec(memory_space=pltpu.SMEM)
    dma = pltpu.SemaphoreType.DMA

    def params(collective):
        return pltpu.CompilerParams(
            collective_id=collective, has_side_effects=True, vmem_limit_bytes=60 * 2**20
        )

    x = pl.pallas_call(
        functools.partial(intersections, n),
        out_shape=jax.ShapeDtypeStruct((n, quarter, width, width), BF16),
        in_specs=[smem, vmem, vmem],
        out_specs=vmem,
        scratch_shapes=[
            pltpu.VMEM((n, pc, rows, width), BF16),
            pltpu.VMEM((n, pc, rows), jnp.int32),
            pltpu.VMEM((pc, width, NB), BF16),
            pltpu.VMEM((pc, NB, width), BF16),
            pltpu.VMEM((2, 2 * quarter, width, width), F32),
            pltpu.VMEM((2, 2 * quarter, width, width), F32),
            pltpu.VMEM((n, 2 * quarter, width, width), F32),
            pltpu.VMEM((2, quarter, width, width), F32),
            pltpu.VMEM((n, quarter, width, width), F32),
            pltpu.VMEM((n, quarter, width, width), F32),
            dma((2, steps, 3)), dma((2, steps, 3)),
            dma((n,)), dma((n,)), dma((n,)), dma((n,)),
        ],
        compiler_params=params(0),
        name="intersections",
    )(slots, coefficients, domain)

    def iterate(first, start):
        shape = (quarter, width, width) if first else (pc, width, width)
        return pl.pallas_call(
            functools.partial(iteration, n, first),
            out_shape=jax.ShapeDtypeStruct(shape, BF16 if first else F32),
            in_specs=[smem, smem, smem, vmem, vmem, vmem, vmem],
            out_specs=vmem,
            scratch_shapes=[
                pltpu.VMEM((n * pc, width, width), BF16),
                pltpu.VMEM((pc, width, width), BF16),
                pltpu.VMEM((quarter, width, width), F32),
                pltpu.VMEM((quarter, width, width), F32),
                pltpu.VMEM((3, quarter, width, width), F32),
                dma((2, steps, 2)), dma((2, steps, 2)),
                dma((n, 2)), dma((n, 2)), dma, dma, dma((3,)), dma((3,)),
            ],
            compiler_params=params(1 if first else 2),
            name="first" if first else "second",
        )(slots, focks, pair_shift.reshape(-1, 1), start, x, exchange_integrals, pno_energy)

    return iterate(False, iterate(True, amplitudes_start))


def solution(mesh):
    placed = (
        P("pairs", "grp", None),
        P("pairs", "grp"),
        P("pairs", None),
        P("pairs", None),
        P("pairs", None),
        P("pairs", None, None),
        P("pairs", None),
        P("pairs"),
        P("pairs", None, None),
    )
    return jax.shard_map(
        on_device, mesh=mesh, in_specs=placed, out_specs=P("pairs", None, None), check_vma=False
    )
```

```python
import functools

import jax
import jax.numpy as jnp
from jax import lax
from jax.experimental import pallas as pl
from jax.experimental.pallas import tpu as pltpu
from jax.sharding import PartitionSpec as P

NB = 192
MESH = pl.DeviceIdType.MESH
F32, BF16 = jnp.float32, jnp.bfloat16


def ring_position(rank, n):
    odd = rank % 2
    return (1 - odd) * (rank // 2) + odd * (n - 1 - rank // 2)


def ring_rank(position, n):
    back = position // (n // 2)
    return (1 - back) * 2 * position + back * (2 * (n - 1 - position) + 1)


def places(n):
    p, g = lax.axis_index("pairs"), lax.axis_index("grp")
    position = ring_position(p, n)
    core, half = g % 2, g // 2
    mate = 2 * half + (1 - core)
    across = 2 * (1 - half) + core
    return p, g, position, mate, across


def at(position, n):
    return ring_rank((position + n) % n, n)


def greet(peers):
    barrier = pltpu.get_barrier_semaphore()
    for peer in peers:
        pl.semaphore_signal(barrier, inc=1, device_id=peer, device_id_type=MESH)
    pl.semaphore_wait(barrier, len(peers))


def remote(src, dst, send, recv, peer):
    return pltpu.make_async_remote_copy(
        src_ref=src, dst_ref=dst, send_sem=send, recv_sem=recv, device_id=peer, device_id_type=MESH
    )


def ring_parts(steps, parts):
    def of(step, direction):
        if step < steps:
            return tuple(range(parts))
        return tuple(c for c in range(parts) if c % 2 == direction)

    return of


def intersections(
    n, slot_ref, c_ref, dom_ref, out_ref,
    cbuf, dbuf, turned, wide, own, msend, mrecv, ysend, yrecv, keep,
    rs, rr, ms, mr, ys, yr,
):
    p, g, position, mate, across = places(n)
    pc = c_ref.shape[0]
    quarter = pc // 4
    rows = c_ref.shape[1]
    steps = n // 2
    right, left = at(position + 1, n), at(position - 1, n)
    ring_peer = (lambda r: (r, g))
    peers = [(right, g), (left, g), (p, mate), (p, across)]
    greet(peers)
    parts_of = ring_parts(steps, 3)
    hp = pc // 2

    def part(ref_c, ref_d, c):
        if c == 2:
            return ref_d
        return ref_c.at[pl.ds(c * hp, hp)]

    def move(step, direction, c):
        offset = -(step - 1) if direction == 0 else step - 1
        rank = at(position + offset, n)
        if step == 1:
            src = part(c_ref, dom_ref, c)
        else:
            src = part(cbuf.at[rank], dbuf.at[rank], c)
        dst = part(cbuf.at[rank], dbuf.at[rank], c)
        return remote(
            src, dst, rs.at[direction, step - 1, c], rr.at[direction, step - 1, c],
            ring_peer(right if direction == 0 else left),
        )

    def arrive(step, direction, c):
        offset = -step if direction == 0 else step
        rank = at(position + offset, n)
        dst = part(cbuf.at[rank], dbuf.at[rank], c)
        remote(
            dst, dst, rs.at[direction, step - 1, c], rr.at[direction, step - 1, c],
            ring_peer(left if direction == 0 else right),
        ).wait_recv()

    for c in (2, 0, 1):
        for d in (0, 1):
            if c in parts_of(1, d):
                move(1, d, c).start()

    base = g * NB
    lines = lax.broadcasted_iota(jnp.int32, (NB, rows), 0)
    core, half = g % 2, g // 2

    def expand(block, doms):
        def one(s, carry):
            hit = (lines == (doms[pl.ds(s, 1), :] - base)).astype(F32).astype(BF16)
            wide[s] = jnp.dot(hit, block[s], preferred_element_type=F32).astype(BF16)
            return carry

        lax.fori_loop(0, pc, one, 0, unroll=8)

    def mate_copy(k, rank):
        return remote(msend.at[k % 2], mrecv.at[rank], ms.at[k], mr.at[k], (p, mate))

    def across_copy(k, rank):
        return remote(ysend.at[k % 2], yrecv.at[rank], ys.at[k], yr.at[k], (p, across))

    ranks = []

    def product(t, rank):
        return jnp.dot(turned[t], wide[slot_ref[t, rank]], preferred_element_type=F32)

    def links(k, rank):
        if k >= 2:
            mate_copy(k - 2, ranks[k - 2]).wait_send()

        def theirs(i, carry):
            t = (2 * (i // quarter) + 1 - core) * quarter + i % quarter
            msend[k % 2, i] = product(t, rank)
            return carry

        lax.fori_loop(0, 2 * quarter, theirs, 0, unroll=8)
        mate_copy(k, rank).start()

        def ours(i, carry):
            t = (2 * (i // quarter) + core) * quarter + i % quarter
            own[k % 2, i] = product(t, rank)
            return carry

        lax.fori_loop(0, 2 * quarter, ours, 0, unroll=8)

    def finish(k):
        rank = ranks[k]
        if k >= 2:
            across_copy(k - 2, ranks[k - 2]).wait_send()
        mate_copy(k, rank).wait_recv()

        def send(j, carry):
            i = (1 - half) * quarter + j
            ysend[k % 2, j] = own[k % 2, i] + mrecv[rank, i]
            return carry

        lax.fori_loop(0, quarter, send, 0)
        across_copy(k, rank).start()

        def hold(j, carry):
            i = half * quarter + j
            keep[rank, j] = own[k % 2, i] + mrecv[rank, i]
            return carry

        lax.fori_loop(0, quarter, hold, 0)

    def process(rank):
        k = len(ranks)
        ranks.append(rank)
        links(k, rank)

    expand(c_ref, dom_ref)

    def turn(t, carry):
        turned[t] = wide[t].astype(F32).T.astype(BF16)
        return carry

    lax.fori_loop(0, pc, turn, 0, unroll=2)
    process(p)
    finish(0)
    for step in range(1, steps + 1):
        for c in (2, 0, 1):
            for d in (0, 1):
                if c in parts_of(step, d):
                    arrive(step, d, c)
                if step < steps and c in parts_of(step + 1, d):
                    move(step + 1, d, c).start()
        for d in (0, 1) if step < steps else (0,):
            rank = at(position + (-step if d == 0 else step), n)
            expand(cbuf.at[rank], dbuf.at[rank])
            process(rank)
            if d == 1:
                finish(len(ranks) - 2)
        finish(len(ranks) - 1)
    for k in range(n):
        rank = ranks[k]
        across_copy(k, rank).wait_recv()

        def last(j, carry):
            out_ref[rank, j] = (keep[rank, j] + yrecv[rank, j]).astype(BF16)
            return carry

        lax.fori_loop(0, quarter, last, 0)
    for k in (n - 2, n - 1):
        mate_copy(k, ranks[k]).wait_send()
        across_copy(k, ranks[k]).wait_send()
    for step in range(1, steps + 1):
        for d in (0, 1):
            for c in parts_of(step, d):
                move(step, d, c).wait_send()


def iteration(
    n, first, slot_ref, fock_ref, start_ref, x_ref, k_ref, e_ref, out_ref,
    abuf, stage, acc, mine, rs, rr, ms, mr, ys, yr, fs, fr,
):
    p, g, position, mate, across = places(n)
    pc = k_ref.shape[0]
    width = k_ref.shape[1]
    quarter = pc // 4
    eighth = quarter // 2
    steps = n // 2
    right, left = at(position + 1, n), at(position - 1, n)
    diagonal = 3 - g
    greet([(right, g), (left, g), (p, mate), (p, across)])
    parts_of = ring_parts(steps, 3)

    def chunk(rank, group, c):
        return abuf.at[pl.ds(rank * pc + group * quarter + (c % 2) * eighth, eighth)]

    def span(rank, c):
        return chunk(rank, g if c < 2 else across, c)

    def ring_copy(step, direction, c):
        offset = -(step - 1) if direction == 0 else step - 1
        ref = span(at(position + offset, n), c)
        src = ref
        if step == 1 and c < 2 and not first:
            src = start_ref.at[pl.ds(c * eighth, eighth)]
        return remote(
            src, ref, rs.at[direction, step - 1, c], rr.at[direction, step - 1, c],
            (right if direction == 0 else left, g),
        )

    def arrive(step, direction, c):
        offset = -step if direction == 0 else step
        ref = span(at(position + offset, n), c)
        remote(
            ref, ref, rs.at[direction, step - 1, c], rr.at[direction, step - 1, c],
            (left if direction == 0 else right, g),
        ).wait_recv()

    def mate_copy(k, rank, c, src=None):
        ref = span(rank, c)
        return remote(ref if src is None else src, ref, ms.at[k, c], mr.at[k, c], (p, mate))

    def mate_wait(k, rank):
        for c in range(4):
            ref = chunk(rank, mate if c < 2 else diagonal, c)
            remote(ref, ref, ms.at[k, c], mr.at[k, c], (p, mate)).wait_recv()

    def across_copy(k, rank, c=1, src=None):
        ref = span(rank, c)
        sem = k if c == 1 else n
        return remote(ref if src is None else src, ref, ys.at[sem], yr.at[sem], (p, across))

    def across_wait(k, rank, c=3):
        ref = span(rank, c)
        sem = k if c == 3 else n
        remote(ref, ref, ys.at[sem], yr.at[sem], (p, across)).wait_recv()

    def own_half(c):
        return start_ref.at[pl.ds(c * eighth, eighth)]

    if first:
        def copy_own(i, carry):
            abuf[p * pc + i] = start_ref[i].astype(BF16)
            return carry

        def group_in(group):
            lax.fori_loop(group * quarter, (group + 1) * quarter, copy_own, 0)

        group_in(g)
        for c in (0, 1):
            for d in (0, 1):
                if c in parts_of(1, d):
                    ring_copy(1, d, c).start()
        group_in(across)
        for d in (0, 1):
            if 2 in parts_of(1, d):
                ring_copy(1, d, 2).start()
        group_in(mate)
        group_in(diagonal)
    else:
        for c in (0, 1):
            across_copy(0, p, c, own_half(c)).start()
            for d in (0, 1):
                if c in parts_of(1, d):
                    ring_copy(1, d, c).start()
        for c in (0, 1):
            mate_copy(0, p, c, own_half(c)).start()

        def copy_own(i, carry):
            abuf[p * pc + g * quarter + i] = start_ref[i]
            return carry

        lax.fori_loop(0, quarter, copy_own, 0)
        across_wait(0, p, 2)
        for d in (0, 1):
            if 2 in parts_of(1, d):
                ring_copy(1, d, 2).start()
        mate_copy(0, p, 2).start()
        across_wait(0, p, 3)
        mate_copy(0, p, 3).start()
        mate_wait(0, p)

    acc[...] = jnp.zeros_like(acc)

    def couple(rank):
        def copy(i, carry):
            stage[i] = abuf[rank * pc + i]
            return carry

        lax.fori_loop(0, pc, copy, 0, unroll=4)

        def one(j, carry):
            t = g * quarter + j
            source = stage[slot_ref[t, rank]]
            x = x_ref[rank, j]
            h = jnp.dot(x, source, preferred_element_type=F32).astype(BF16)
            y = lax.dot_general(h, x, (((1,), (1,)), ((), ())), preferred_element_type=F32)
            acc[j] += fock_ref[t, rank] * y
            return carry

        lax.fori_loop(0, quarter, one, 0, unroll=4)

    couple(p)

    def exchange(blocks):
        for k, rank in blocks:
            across_wait(k, rank)
            mate_copy(k, rank, 3).start()

    def use(blocks):
        for k, rank in blocks:
            mate_wait(k, rank)
            couple(rank)

    landed, shared = [], []
    for step in range(1, steps + 1):
        for c in (1, 0, 2):
            for d in (0, 1):
                rank = at(position + (-step if d == 0 else step), n)
                if c in parts_of(step, d):
                    arrive(step, d, c)
                    if step < steps and c in parts_of(step + 1, d):
                        ring_copy(step + 1, d, c).start()
                    k = 2 * step - 1 + (d if step < steps else 0)
                    if c == 1:
                        across_copy(k, rank).start()
                    mate_copy(k, rank, c).start()
        exchange(landed)
        use(shared)
        shared = landed
        landed = [
            (2 * step - 1 + d, at(position + (-step if d == 0 else step), n))
            for d in ((0, 1) if step < steps else (0,))
        ]
    exchange(landed)
    use(shared)
    use(landed)

    def scaled(j):
        t = g * quarter + j
        row = jnp.broadcast_to(e_ref[pl.ds(t, 1), :], (width, width))
        return (-(k_ref[t] + acc[j]) / (row.T + row + fock_ref[t, n])).astype(BF16)

    if first:
        def result(j, carry):
            out_ref[j] = scaled(j)
            return carry

        lax.fori_loop(0, quarter, result, 0, unroll=2)
    else:
        def block(ref, group):
            return ref.at[pl.ds(group * quarter, quarter)]

        def result(j, carry):
            value = scaled(j)
            mine[j] = value
            out_ref[g * quarter + j] = value
            return carry

        lax.fori_loop(0, quarter, result, 0, unroll=2)
        over = remote(mine, block(out_ref, g), fs.at[0], fr.at[0], (p, across))
        beside = remote(mine, block(out_ref, g), fs.at[1], fr.at[1], (p, mate))
        corner = remote(
            block(out_ref, across), block(out_ref, across), fs.at[2], fr.at[2], (p, mate)
        )
        over.start()
        beside.start()
        remote(mine, block(out_ref, across), fs.at[0], fr.at[0], (p, across)).wait_recv()
        corner.start()
        remote(mine, block(out_ref, mate), fs.at[1], fr.at[1], (p, mate)).wait_recv()
        remote(mine, block(out_ref, diagonal), fs.at[2], fr.at[2], (p, mate)).wait_recv()
        over.wait_send()
        beside.wait_send()
        corner.wait_send()
        across_copy(0, p, 0, own_half(0)).wait_send()
        across_copy(0, p, 1, own_half(1)).wait_send()
        for c in range(4):
            mate_copy(0, p, c).wait_send()
    for k in range(1, n):
        across_copy(k, p).wait_send()
        for c in range(4):
            mate_copy(k, p, c).wait_send()
    for step in range(1, steps + 1):
        for d in (0, 1):
            for c in parts_of(step, d):
                ring_copy(step, d, c).wait_send()


def on_device(
    coefficients, domain, coupling_owner, coupling_slot, coupling_fock,
    exchange_integrals, pno_energy, pair_shift, amplitudes_start,
):
    n = lax.axis_size("pairs")
    pc, rows, width = coefficients.shape
    quarter = pc // lax.axis_size("grp")
    steps = n // 2
    named = coupling_owner[:, :, None] == jnp.arange(n, dtype=jnp.int32)[None, None, :]
    slots = jnp.sum(jnp.where(named, coupling_slot[:, :, None], 0), axis=1)
    focks = jnp.sum(jnp.where(named, coupling_fock[:, :, None], 0.0), axis=1)
    focks = jnp.concatenate([focks, pair_shift[:, None]], axis=1)
    vmem, smem = pl.BlockSpec(memory_space=pltpu.VMEM), pl.BlockSpec(memory_space=pltpu.SMEM)
    dma = pltpu.SemaphoreType.DMA

    def params(collective):
        return pltpu.CompilerParams(
            collective_id=collective, has_side_effects=True, vmem_limit_bytes=60 * 2**20
        )

    x = pl.pallas_call(
        functools.partial(intersections, n),
        out_shape=jax.ShapeDtypeStruct((n, quarter, width, width), BF16),
        in_specs=[smem, vmem, vmem],
        out_specs=vmem,
        scratch_shapes=[
            pltpu.VMEM((n, pc, rows, width), BF16),
            pltpu.VMEM((n, pc, rows), jnp.int32),
            pltpu.VMEM((pc, width, NB), BF16),
            pltpu.VMEM((pc, NB, width), BF16),
            pltpu.VMEM((2, 2 * quarter, width, width), F32),
            pltpu.VMEM((2, 2 * quarter, width, width), F32),
            pltpu.VMEM((n, 2 * quarter, width, width), F32),
            pltpu.VMEM((2, quarter, width, width), F32),
            pltpu.VMEM((n, quarter, width, width), F32),
            pltpu.VMEM((n, quarter, width, width), F32),
            dma((2, steps, 3)), dma((2, steps, 3)),
            dma((n,)), dma((n,)), dma((n,)), dma((n,)),
        ],
        compiler_params=params(0),
        name="intersections",
    )(slots, coefficients, domain)

    def iterate(first, start):
        shape = (quarter, width, width) if first else (pc, width, width)
        return pl.pallas_call(
            functools.partial(iteration, n, first),
            out_shape=jax.ShapeDtypeStruct(shape, BF16),
            in_specs=[smem, smem, vmem, vmem, vmem, vmem],
            out_specs=vmem,
            scratch_shapes=[
                pltpu.VMEM((n * pc, width, width), BF16),
                pltpu.VMEM((pc, width, width), BF16),
                pltpu.VMEM((quarter, width, width), F32),
                pltpu.VMEM((quarter, width, width), BF16),
                dma((2, steps, 3)), dma((2, steps, 3)),
                dma((n, 4)), dma((n, 4)), dma((n + 1,)), dma((n + 1,)), dma((3,)), dma((3,)),
            ],
            compiler_params=params(1 if first else 2),
            name="first" if first else "second",
        )(slots, focks, start, x, exchange_integrals, pno_energy)

    return iterate(False, iterate(True, amplitudes_start)).astype(F32)


def solution(mesh):
    placed = (
        P("pairs", "grp", None),
        P("pairs", "grp"),
        P("pairs", None),
        P("pairs", None),
        P("pairs", None),
        P("pairs", None, None),
        P("pairs", None),
        P("pairs"),
        P("pairs", None, None),
    )
    return jax.shard_map(
        on_device, mesh=mesh, in_specs=placed, out_specs=P("pairs", None, None), check_vma=False
    )
```

```python
import functools

import jax
import jax.numpy as jnp
from jax import lax
from jax.experimental import pallas as pl
from jax.experimental.pallas import tpu as pltpu
from jax.sharding import PartitionSpec as P

NB = 192
MESH = pl.DeviceIdType.MESH
F32, BF16 = jnp.float32, jnp.bfloat16


def ring_position(rank, n):
    odd = rank % 2
    return (1 - odd) * (rank // 2) + odd * (n - 1 - rank // 2)


def ring_rank(position, n):
    back = position // (n // 2)
    return (1 - back) * 2 * position + back * (2 * (n - 1 - position) + 1)


def places(n):
    p, g = lax.axis_index("pairs"), lax.axis_index("grp")
    position = ring_position(p, n)
    core, half = g % 2, g // 2
    mate = 2 * half + (1 - core)
    across = 2 * (1 - half) + core
    return p, g, position, mate, across


def at(position, n):
    return ring_rank((position + n) % n, n)


def greet(peers):
    barrier = pltpu.get_barrier_semaphore()
    for peer in peers:
        pl.semaphore_signal(barrier, inc=1, device_id=peer, device_id_type=MESH)
    pl.semaphore_wait(barrier, len(peers))


def remote(src, dst, send, recv, peer):
    return pltpu.make_async_remote_copy(
        src_ref=src, dst_ref=dst, send_sem=send, recv_sem=recv, device_id=peer, device_id_type=MESH
    )


def ring_parts(steps, parts):
    def of(step, direction):
        if step < steps:
            return tuple(range(parts))
        return tuple(c for c in range(parts) if c % 2 == direction)

    return of


def intersections(
    n, slot_ref, c_ref, dom_ref, out_ref,
    cbuf, dbuf, turned, wide, own, msend, mrecv, ysend, yrecv, keep,
    rs, rr, ms, mr, ys, yr,
):
    p, g, position, mate, across = places(n)
    pc = c_ref.shape[0]
    quarter = pc // 4
    rows = c_ref.shape[1]
    steps = n // 2
    right, left = at(position + 1, n), at(position - 1, n)
    ring_peer = (lambda r: (r, g))
    peers = [(right, g), (left, g), (p, mate), (p, across)]
    greet(peers)
    parts_of = ring_parts(steps, 3)
    hp = pc // 2

    def part(ref_c, ref_d, c):
        if c == 2:
            return ref_d
        return ref_c.at[pl.ds(c * hp, hp)]

    def move(step, direction, c):
        offset = -(step - 1) if direction == 0 else step - 1
        rank = at(position + offset, n)
        if step == 1:
            src = part(c_ref, dom_ref, c)
        else:
            src = part(cbuf.at[rank], dbuf.at[rank], c)
        dst = part(cbuf.at[rank], dbuf.at[rank], c)
        return remote(
            src, dst, rs.at[direction, step - 1, c], rr.at[direction, step - 1, c],
            ring_peer(right if direction == 0 else left),
        )

    def arrive(step, direction, c):
        offset = -step if direction == 0 else step
        rank = at(position + offset, n)
        dst = part(cbuf.at[rank], dbuf.at[rank], c)
        remote(
            dst, dst, rs.at[direction, step - 1, c], rr.at[direction, step - 1, c],
            ring_peer(left if direction == 0 else right),
        ).wait_recv()

    for c in (2, 0, 1):
        for d in (0, 1):
            if c in parts_of(1, d):
                move(1, d, c).start()

    base = g * NB
    lines = lax.broadcasted_iota(jnp.int32, (NB, rows), 0)
    core, half = g % 2, g // 2

    def expand(block, doms):
        def one(s, carry):
            hit = (lines == (doms[pl.ds(s, 1), :] - base)).astype(F32).astype(BF16)
            wide[s] = jnp.dot(hit, block[s], preferred_element_type=F32).astype(BF16)
            return carry

        lax.fori_loop(0, pc, one, 0, unroll=8)

    def mate_copy(k, rank):
        return remote(msend.at[k % 2], mrecv.at[rank], ms.at[k], mr.at[k], (p, mate))

    def across_copy(k, rank):
        return remote(ysend.at[k % 2], yrecv.at[rank], ys.at[k], yr.at[k], (p, across))

    ranks = []

    def product(t, rank):
        return jnp.dot(turned[t], wide[slot_ref[t, rank]], preferred_element_type=F32)

    def links(k, rank):
        if k >= 2:
            mate_copy(k - 2, ranks[k - 2]).wait_send()

        def theirs(i, carry):
            t = (2 * (i // quarter) + 1 - core) * quarter + i % quarter
            msend[k % 2, i] = product(t, rank)
            return carry

        lax.fori_loop(0, 2 * quarter, theirs, 0, unroll=8)
        mate_copy(k, rank).start()

        def ours(i, carry):
            t = (2 * (i // quarter) + core) * quarter + i % quarter
            own[k % 2, i] = product(t, rank)
            return carry

        lax.fori_loop(0, 2 * quarter, ours, 0, unroll=8)

    def finish(k):
        rank = ranks[k]
        if k >= 2:
            across_copy(k - 2, ranks[k - 2]).wait_send()
        mate_copy(k, rank).wait_recv()

        def send(j, carry):
            i = (1 - half) * quarter + j
            ysend[k % 2, j] = own[k % 2, i] + mrecv[rank, i]
            return carry

        lax.fori_loop(0, quarter, send, 0)
        across_copy(k, rank).start()

        def hold(j, carry):
            i = half * quarter + j
            keep[rank, j] = own[k % 2, i] + mrecv[rank, i]
            return carry

        lax.fori_loop(0, quarter, hold, 0)

    def process(rank):
        k = len(ranks)
        ranks.append(rank)
        links(k, rank)

    expand(c_ref, dom_ref)

    def turn(t, carry):
        turned[t] = wide[t].astype(F32).T.astype(BF16)
        return carry

    lax.fori_loop(0, pc, turn, 0, unroll=2)
    process(p)
    finish(0)
    for step in range(1, steps + 1):
        for c in (2, 0, 1):
            for d in (0, 1):
                if c in parts_of(step, d):
                    arrive(step, d, c)
                if step < steps and c in parts_of(step + 1, d):
                    move(step + 1, d, c).start()
        if step == steps - 1:
            yield None
        for d in (0, 1) if step < steps else (0,):
            rank = at(position + (-step if d == 0 else step), n)
            expand(cbuf.at[rank], dbuf.at[rank])
            process(rank)
            if d == 1:
                finish(len(ranks) - 2)
        finish(len(ranks) - 1)
    def settle(k):
        rank = ranks[k]
        across_copy(k, rank).wait_recv()

        def last(j, carry):
            out_ref[rank, j] = (keep[rank, j] + yrecv[rank, j]).astype(BF16)
            return carry

        lax.fori_loop(0, quarter, last, 0)

    yield settle
    for k in (n - 2, n - 1):
        mate_copy(k, ranks[k]).wait_send()
        across_copy(k, ranks[k]).wait_send()
    for step in range(1, steps + 1):
        for d in (0, 1):
            for c in parts_of(step, d):
                move(step, d, c).wait_send()


def iteration(
    n, first, joined, slot_ref, fock_ref, start_ref, x_ref, k_ref, e_ref, out_ref,
    abuf, stage, acc, mine, rs, rr, ms, mr, ys, yr, fs, fr,
):
    p, g, position, mate, across = places(n)
    pc = k_ref.shape[0]
    width = k_ref.shape[1]
    quarter = pc // 4
    eighth = quarter // 2
    steps = n // 2
    right, left = at(position + 1, n), at(position - 1, n)
    diagonal = 3 - g
    if not joined:
        greet([(right, g), (left, g), (p, mate), (p, across)])
    parts = 4 if joined else 3
    parts_of = ring_parts(steps, parts)

    def chunk(rank, group, c):
        return abuf.at[pl.ds(rank * pc + group * quarter + (c % 2) * eighth, eighth)]

    def span(rank, c):
        return chunk(rank, g if c < 2 else across, c)

    def ring_copy(step, direction, c):
        offset = -(step - 1) if direction == 0 else step - 1
        ref = span(at(position + offset, n), c)
        src = ref
        if step == 1 and c < 2 and not first:
            src = start_ref.at[pl.ds(c * eighth, eighth)]
        return remote(
            src, ref, rs.at[direction, step - 1, c], rr.at[direction, step - 1, c],
            (right if direction == 0 else left, g),
        )

    def arrive(step, direction, c):
        offset = -step if direction == 0 else step
        ref = span(at(position + offset, n), c)
        remote(
            ref, ref, rs.at[direction, step - 1, c], rr.at[direction, step - 1, c],
            (left if direction == 0 else right, g),
        ).wait_recv()

    def mate_copy(k, rank, c, src=None):
        ref = span(rank, c)
        return remote(ref if src is None else src, ref, ms.at[k, c], mr.at[k, c], (p, mate))

    def mate_wait(k, rank):
        for c in range(4):
            ref = chunk(rank, mate if c < 2 else diagonal, c)
            remote(ref, ref, ms.at[k, c], mr.at[k, c], (p, mate)).wait_recv()

    def across_copy(k, rank, c=1, src=None):
        ref = span(rank, c)
        sem = k if c == 1 else n
        return remote(ref if src is None else src, ref, ys.at[sem], yr.at[sem], (p, across))

    def across_wait(k, rank, c=3):
        ref = span(rank, c)
        sem = k if c == 3 else n
        remote(ref, ref, ys.at[sem], yr.at[sem], (p, across)).wait_recv()

    def own_half(c):
        return start_ref.at[pl.ds(c * eighth, eighth)]

    if first:
        def copy_own(i, carry):
            abuf[p * pc + i] = start_ref[i].astype(BF16)
            return carry

        def group_in(group):
            lax.fori_loop(group * quarter, (group + 1) * quarter, copy_own, 0)

        group_in(g)
        for c in (0, 1):
            for d in (0, 1):
                if c in parts_of(1, d):
                    ring_copy(1, d, c).start()
        group_in(across)
        for c in range(2, parts):
            for d in (0, 1):
                if c in parts_of(1, d):
                    ring_copy(1, d, c).start()
        group_in(mate)
        group_in(diagonal)
    else:
        for c in (0, 1):
            across_copy(0, p, c, own_half(c)).start()
            for d in (0, 1):
                if c in parts_of(1, d):
                    ring_copy(1, d, c).start()
        for c in (0, 1):
            mate_copy(0, p, c, own_half(c)).start()

        def copy_own(i, carry):
            abuf[p * pc + g * quarter + i] = start_ref[i]
            return carry

        lax.fori_loop(0, quarter, copy_own, 0)
        across_wait(0, p, 2)
        for d in (0, 1):
            if 2 in parts_of(1, d):
                ring_copy(1, d, 2).start()
        mate_copy(0, p, 2).start()
        across_wait(0, p, 3)
        mate_copy(0, p, 3).start()
        mate_wait(0, p)

    settle = yield None
    acc[...] = jnp.zeros_like(acc)

    def couple(rank, k):
        if settle is not None:
            settle(k)

        def copy(i, carry):
            stage[i] = abuf[rank * pc + i]
            return carry

        lax.fori_loop(0, pc, copy, 0, unroll=4)

        def one(j, carry):
            t = g * quarter + j
            source = stage[slot_ref[t, rank]]
            x = x_ref[rank, j]
            h = jnp.dot(x, source, preferred_element_type=F32).astype(BF16)
            y = lax.dot_general(h, x, (((1,), (1,)), ((), ())), preferred_element_type=F32)
            acc[j] += fock_ref[t, rank] * y
            return carry

        lax.fori_loop(0, quarter, one, 0, unroll=4)

    couple(p, 0)

    def exchange(blocks):
        for k, rank in () if joined else blocks:
            across_wait(k, rank)
            mate_copy(k, rank, 3).start()

    def use(blocks):
        for k, rank in blocks:
            mate_wait(k, rank)
            couple(rank, k)

    landed, shared = [], []
    for step in range(1, steps + 1):
        for c in (1, 0, 2, 3)[:parts]:
            for d in (0, 1):
                rank = at(position + (-step if d == 0 else step), n)
                if c in parts_of(step, d):
                    arrive(step, d, c)
                    if step < steps and c in parts_of(step + 1, d):
                        ring_copy(step + 1, d, c).start()
                    k = 2 * step - 1 + (d if step < steps else 0)
                    if c == 1 and not joined:
                        across_copy(k, rank).start()
                    mate_copy(k, rank, c).start()
        exchange(landed)
        use(shared)
        shared = landed
        landed = [
            (2 * step - 1 + d, at(position + (-step if d == 0 else step), n))
            for d in ((0, 1) if step < steps else (0,))
        ]
    exchange(landed)
    use(shared)
    use(landed)

    def scaled(j):
        t = g * quarter + j
        row = jnp.broadcast_to(e_ref[pl.ds(t, 1), :], (width, width))
        return (-(k_ref[t] + acc[j]) / (row.T + row + fock_ref[t, n])).astype(BF16)

    if first:
        def result(j, carry):
            out_ref[j] = scaled(j)
            return carry

        lax.fori_loop(0, quarter, result, 0, unroll=2)
    else:
        def block(ref, group):
            return ref.at[pl.ds(group * quarter, quarter)]

        def result(j, carry):
            value = scaled(j)
            mine[j] = value
            out_ref[g * quarter + j] = value
            return carry

        lax.fori_loop(0, quarter, result, 0, unroll=2)
        over = remote(mine, block(out_ref, g), fs.at[0], fr.at[0], (p, across))
        beside = remote(mine, block(out_ref, g), fs.at[1], fr.at[1], (p, mate))
        corner = remote(
            block(out_ref, across), block(out_ref, across), fs.at[2], fr.at[2], (p, mate)
        )
        over.start()
        beside.start()
        remote(mine, block(out_ref, across), fs.at[0], fr.at[0], (p, across)).wait_recv()
        corner.start()
        remote(mine, block(out_ref, mate), fs.at[1], fr.at[1], (p, mate)).wait_recv()
        remote(mine, block(out_ref, diagonal), fs.at[2], fr.at[2], (p, mate)).wait_recv()
        over.wait_send()
        beside.wait_send()
        corner.wait_send()
        across_copy(0, p, 0, own_half(0)).wait_send()
        across_copy(0, p, 1, own_half(1)).wait_send()
        for c in range(4):
            mate_copy(0, p, c).wait_send()
    for k in range(1, n):
        if not joined:
            across_copy(k, p).wait_send()
        for c in range(4):
            mate_copy(k, p, c).wait_send()
    for step in range(1, steps + 1):
        for d in (0, 1):
            for c in parts_of(step, d):
                ring_copy(step, d, c).wait_send()


def intersections_alone(*args):
    steps = intersections(*args)
    next(steps)
    settle = next(steps)
    for k in range(args[0]):
        settle(k)
    next(steps, None)


def iteration_alone(n, first, *args):
    steps = iteration(n, first, False, *args)
    next(steps)
    try:
        steps.send(None)
    except StopIteration:
        pass


def opening(
    n, made, slot_ref, fock_ref, c_ref, dom_ref, start_ref, k_ref, e_ref, x_ref, out_ref, *scratch
):
    blocks = intersections(n, slot_ref, c_ref, dom_ref, x_ref, *scratch[:made])
    next(blocks)
    amps = iteration(
        n, True, True, slot_ref, fock_ref, start_ref, x_ref, k_ref, e_ref, out_ref, *scratch[made:]
    )
    next(amps)
    settle = next(blocks)
    try:
        amps.send(settle)
    except StopIteration:
        pass
    next(blocks, None)


def on_device(
    coefficients, domain, coupling_owner, coupling_slot, coupling_fock,
    exchange_integrals, pno_energy, pair_shift, amplitudes_start,
):
    n = lax.axis_size("pairs")
    pc, rows, width = coefficients.shape
    quarter = pc // lax.axis_size("grp")
    steps = n // 2
    named = coupling_owner[:, :, None] == jnp.arange(n, dtype=jnp.int32)[None, None, :]
    slots = jnp.sum(jnp.where(named, coupling_slot[:, :, None], 0), axis=1)
    focks = jnp.sum(jnp.where(named, coupling_fock[:, :, None], 0.0), axis=1)
    focks = jnp.concatenate([focks, pair_shift[:, None]], axis=1)
    vmem, smem = pl.BlockSpec(memory_space=pltpu.VMEM), pl.BlockSpec(memory_space=pltpu.SMEM)
    dma = pltpu.SemaphoreType.DMA

    def params(collective):
        return pltpu.CompilerParams(
            collective_id=collective, has_side_effects=True, vmem_limit_bytes=60 * 2**20
        )

    big = (width, width)
    x_shape = jax.ShapeDtypeStruct((n, quarter, *big), BF16)
    block_scratch = [
        pltpu.VMEM((n, pc, rows, width), BF16),
        pltpu.VMEM((n, pc, rows), jnp.int32),
        pltpu.VMEM((pc, width, NB), BF16),
        pltpu.VMEM((pc, NB, width), BF16),
        pltpu.VMEM((2, 2 * quarter, *big), F32),
        pltpu.VMEM((2, 2 * quarter, *big), F32),
        pltpu.VMEM((n, 2 * quarter, *big), F32),
        pltpu.VMEM((2, quarter, *big), F32),
        pltpu.VMEM((n, quarter, *big), F32),
        pltpu.VMEM((n, quarter, *big), F32),
        dma((2, steps, 3)), dma((2, steps, 3)),
        dma((n,)), dma((n,)), dma((n,)), dma((n,)),
    ]
    amp_scratch = [
        pltpu.VMEM((n * pc, *big), BF16),
        pltpu.VMEM((pc, *big), BF16),
        pltpu.VMEM((quarter, *big), F32),
        pltpu.VMEM((quarter, *big), BF16),
        dma((2, steps, 4)), dma((2, steps, 4)),
        dma((n, 4)), dma((n, 4)), dma((n + 1,)), dma((n + 1,)), dma((3,)), dma((3,)),
    ]
    half_shape = jax.ShapeDtypeStruct((quarter, *big), BF16)

    def iterate(first, start, x):
        return pl.pallas_call(
            functools.partial(iteration_alone, n, first),
            out_shape=half_shape if first else jax.ShapeDtypeStruct((pc, *big), BF16),
            in_specs=[smem, smem, vmem, vmem, vmem, vmem],
            out_specs=vmem,
            scratch_shapes=amp_scratch,
            compiler_params=params(1 if first else 2),
            name="first" if first else "second",
        )(slots, focks, start, x, exchange_integrals, pno_energy)

    held = n * width * (2 * pc * (rows + width) + 4 * width * 4 * quarter + 2 * width * quarter)
    if held < 40 * 2**20:
        x, amps = pl.pallas_call(
            functools.partial(opening, n, len(block_scratch)),
            out_shape=(x_shape, half_shape),
            in_specs=[smem, smem, vmem, vmem, vmem, vmem, vmem],
            out_specs=(vmem, vmem),
            scratch_shapes=block_scratch + amp_scratch,
            compiler_params=params(0),
            name="opening",
        )(slots, focks, coefficients, domain, amplitudes_start, exchange_integrals, pno_energy)
    else:
        x = pl.pallas_call(
            functools.partial(intersections_alone, n),
            out_shape=x_shape,
            in_specs=[smem, vmem, vmem],
            out_specs=vmem,
            scratch_shapes=block_scratch,
            compiler_params=params(0),
            name="intersections",
        )(slots, coefficients, domain)
        amps = iterate(True, amplitudes_start, x)
    return iterate(False, amps, x).astype(F32)


def solution(mesh):
    placed = (
        P("pairs", "grp", None),
        P("pairs", "grp"),
        P("pairs", None),
        P("pairs", None),
        P("pairs", None),
        P("pairs", None, None),
        P("pairs", None),
        P("pairs"),
        P("pairs", None, None),
    )
    return jax.shard_map(
        on_device, mesh=mesh, in_specs=placed, out_specs=P("pairs", None, None), check_vma=False
    )
```

```python
import functools

import jax
import jax.numpy as jnp
from jax import lax
from jax.experimental import pallas as pl
from jax.experimental.pallas import tpu as pltpu
from jax.sharding import PartitionSpec as P

NB = 192
MESH = pl.DeviceIdType.MESH
F32, BF16 = jnp.float32, jnp.bfloat16


def ring_position(rank, n):
    odd = rank % 2
    return (1 - odd) * (rank // 2) + odd * (n - 1 - rank // 2)


def ring_rank(position, n):
    back = position // (n // 2)
    return (1 - back) * 2 * position + back * (2 * (n - 1 - position) + 1)


def places(n):
    p, g = lax.axis_index("pairs"), lax.axis_index("grp")
    position = ring_position(p, n)
    core, half = g % 2, g // 2
    mate = 2 * half + (1 - core)
    across = 2 * (1 - half) + core
    return p, g, position, mate, across


def at(position, n):
    return ring_rank((position + n) % n, n)


def greet(peers):
    barrier = pltpu.get_barrier_semaphore()
    for peer in peers:
        pl.semaphore_signal(barrier, inc=1, device_id=peer, device_id_type=MESH)
    pl.semaphore_wait(barrier, len(peers))


def remote(src, dst, send, recv, peer):
    return pltpu.make_async_remote_copy(
        src_ref=src, dst_ref=dst, send_sem=send, recv_sem=recv, device_id=peer, device_id_type=MESH
    )


def ring_parts(steps, parts):
    def of(step, direction):
        if step < steps:
            return tuple(range(parts))
        return tuple(c for c in range(parts) if c % 2 == direction)

    return of


def intersections(
    n, slot_ref, c_ref, dom_ref, out_ref,
    cbuf, dbuf, turned, wide, own, msend, mrecv, ysend, yrecv, keep,
    rs, rr, ms, mr, ys, yr,
):
    p, g, position, mate, across = places(n)
    pc = c_ref.shape[0]
    quarter = pc // 4
    rows = c_ref.shape[1]
    steps = n // 2
    right, left = at(position + 1, n), at(position - 1, n)
    ring_peer = (lambda r: (r, g))
    peers = [(right, g), (left, g), (p, mate), (p, across)]
    greet(peers)
    parts_of = ring_parts(steps, 3)
    hp = pc // 2

    def part(ref_c, ref_d, c):
        if c == 2:
            return ref_d
        return ref_c.at[pl.ds(c * hp, hp)]

    def move(step, direction, c):
        offset = -(step - 1) if direction == 0 else step - 1
        rank = at(position + offset, n)
        if step == 1:
            src = part(c_ref, dom_ref, c)
        else:
            src = part(cbuf.at[rank], dbuf.at[rank], c)
        dst = part(cbuf.at[rank], dbuf.at[rank], c)
        return remote(
            src, dst, rs.at[direction, step - 1, c], rr.at[direction, step - 1, c],
            ring_peer(right if direction == 0 else left),
        )

    def arrive(step, direction, c):
        offset = -step if direction == 0 else step
        rank = at(position + offset, n)
        dst = part(cbuf.at[rank], dbuf.at[rank], c)
        remote(
            dst, dst, rs.at[direction, step - 1, c], rr.at[direction, step - 1, c],
            ring_peer(left if direction == 0 else right),
        ).wait_recv()

    for c in (2, 0, 1):
        for d in (0, 1):
            if c in parts_of(1, d):
                move(1, d, c).start()

    base = g * NB
    lines = lax.broadcasted_iota(jnp.int32, (NB, rows), 0)
    core, half = g % 2, g // 2

    def expand(block, doms):
        def one(s, carry):
            hit = (lines == (doms[pl.ds(s, 1), :] - base)).astype(F32).astype(BF16)
            wide[s] = jnp.dot(hit, block[s], preferred_element_type=F32).astype(BF16)
            return carry

        lax.fori_loop(0, pc, one, 0, unroll=8)

    def mate_copy(k, rank):
        return remote(msend.at[k % 2], mrecv.at[rank], ms.at[k], mr.at[k], (p, mate))

    def across_copy(k, rank):
        return remote(ysend.at[k % 2], yrecv.at[rank], ys.at[k], yr.at[k], (p, across))

    ranks = []

    def product(t, rank):
        return jnp.dot(turned[t], wide[slot_ref[t, rank]], preferred_element_type=F32)

    def links(k, rank):
        if k >= 2:
            mate_copy(k - 2, ranks[k - 2]).wait_send()

        def theirs(i, carry):
            t = (2 * (i // quarter) + 1 - core) * quarter + i % quarter
            msend[k % 2, i] = product(t, rank)
            return carry

        lax.fori_loop(0, 2 * quarter, theirs, 0, unroll=8)
        mate_copy(k, rank).start()

        def ours(i, carry):
            t = (2 * (i // quarter) + core) * quarter + i % quarter
            own[k % 2, i] = product(t, rank)
            return carry

        lax.fori_loop(0, 2 * quarter, ours, 0, unroll=8)

    def finish(k):
        rank = ranks[k]
        if k >= 2:
            across_copy(k - 2, ranks[k - 2]).wait_send()
        mate_copy(k, rank).wait_recv()

        def send(j, carry):
            i = (1 - half) * quarter + j
            ysend[k % 2, j] = own[k % 2, i] + mrecv[rank, i]
            return carry

        lax.fori_loop(0, quarter, send, 0)
        across_copy(k, rank).start()

        def hold(j, carry):
            i = half * quarter + j
            keep[rank, j] = own[k % 2, i] + mrecv[rank, i]
            return carry

        lax.fori_loop(0, quarter, hold, 0)

    def process(rank):
        k = len(ranks)
        ranks.append(rank)
        links(k, rank)

    expand(c_ref, dom_ref)

    def turn(t, carry):
        turned[t] = wide[t].astype(F32).T.astype(BF16)
        return carry

    lax.fori_loop(0, pc, turn, 0, unroll=2)
    process(p)
    finish(0)
    for step in range(1, steps + 1):
        for c in (2, 0, 1):
            for d in (0, 1):
                if c in parts_of(step, d):
                    arrive(step, d, c)
                if step < steps and c in parts_of(step + 1, d):
                    move(step + 1, d, c).start()
        if step == steps - 1:
            yield None
        for d in (0, 1) if step < steps else (0,):
            rank = at(position + (-step if d == 0 else step), n)
            expand(cbuf.at[rank], dbuf.at[rank])
            process(rank)
            if d == 1:
                finish(len(ranks) - 2)
        finish(len(ranks) - 1)
    def settle(k):
        rank = ranks[k]
        across_copy(k, rank).wait_recv()

        def last(j, carry):
            out_ref[rank, j] = (keep[rank, j] + yrecv[rank, j]).astype(BF16)
            return carry

        lax.fori_loop(0, quarter, last, 0)

    yield settle
    for k in (n - 2, n - 1):
        mate_copy(k, ranks[k]).wait_send()
        across_copy(k, ranks[k]).wait_send()
    for step in range(1, steps + 1):
        for d in (0, 1):
            for c in parts_of(step, d):
                move(step, d, c).wait_send()


def iteration(
    n, first, joined, alone, slot_ref, fock_ref, start_ref, x_ref, k_ref, e_ref, out_ref,
    abuf, stage, acc, mine, rs, rr, ms, mr, ys, yr, fs, fr,
):
    p, g, position, mate, across = places(n)
    pc = k_ref.shape[0]
    width = k_ref.shape[1]
    quarter = pc // 4
    eighth = quarter // 2
    steps = n // 2
    right, left = at(position + 1, n), at(position - 1, n)
    diagonal = 3 - g
    if alone:
        greet([(right, g), (left, g), (p, mate), (p, across)])
    parts = 4 if joined else 3
    parts_of = ring_parts(steps, parts)

    def chunk(rank, group, c):
        return abuf.at[pl.ds(rank * pc + group * quarter + (c % 2) * eighth, eighth)]

    def span(rank, c):
        return chunk(rank, g if c < 2 else across, c)

    def ring_copy(step, direction, c):
        offset = -(step - 1) if direction == 0 else step - 1
        ref = span(at(position + offset, n), c)
        src = ref
        if step == 1 and c < 2 and not first:
            src = start_ref.at[pl.ds(c * eighth, eighth)]
        return remote(
            src, ref, rs.at[direction, step - 1, c], rr.at[direction, step - 1, c],
            (right if direction == 0 else left, g),
        )

    def arrive(step, direction, c):
        offset = -step if direction == 0 else step
        ref = span(at(position + offset, n), c)
        remote(
            ref, ref, rs.at[direction, step - 1, c], rr.at[direction, step - 1, c],
            (left if direction == 0 else right, g),
        ).wait_recv()

    def mate_copy(k, rank, c, src=None):
        ref = span(rank, c)
        return remote(ref if src is None else src, ref, ms.at[k, c], mr.at[k, c], (p, mate))

    def mate_wait(k, rank):
        for c in range(4):
            ref = chunk(rank, mate if c < 2 else diagonal, c)
            remote(ref, ref, ms.at[k, c], mr.at[k, c], (p, mate)).wait_recv()

    def across_copy(k, rank, c=1, src=None):
        ref = span(rank, c)
        sem = k if c == 1 else n
        return remote(ref if src is None else src, ref, ys.at[sem], yr.at[sem], (p, across))

    def across_wait(k, rank, c=3):
        ref = span(rank, c)
        sem = k if c == 3 else n
        remote(ref, ref, ys.at[sem], yr.at[sem], (p, across)).wait_recv()

    def own_half(c):
        return start_ref.at[pl.ds(c * eighth, eighth)]

    if first:
        def copy_own(i, carry):
            abuf[p * pc + i] = start_ref[i].astype(BF16)
            return carry

        def group_in(group):
            lax.fori_loop(group * quarter, (group + 1) * quarter, copy_own, 0)

        group_in(g)
        for c in (0, 1):
            for d in (0, 1):
                if c in parts_of(1, d):
                    ring_copy(1, d, c).start()
        group_in(across)
        for c in range(2, parts):
            for d in (0, 1):
                if c in parts_of(1, d):
                    ring_copy(1, d, c).start()
        group_in(mate)
        group_in(diagonal)
    else:
        for c in (0, 1):
            across_copy(0, p, c, own_half(c)).start()
            for d in (0, 1):
                if c in parts_of(1, d):
                    ring_copy(1, d, c).start()
        for c in (0, 1):
            mate_copy(0, p, c, own_half(c)).start()

        def copy_own(i, carry):
            abuf[p * pc + g * quarter + i] = start_ref[i]
            return carry

        lax.fori_loop(0, quarter, copy_own, 0)
        across_wait(0, p, 2)
        for d in (0, 1):
            if 2 in parts_of(1, d):
                ring_copy(1, d, 2).start()
        mate_copy(0, p, 2).start()
        across_wait(0, p, 3)
        mate_copy(0, p, 3).start()
        mate_wait(0, p)

    settle = yield None
    acc[...] = jnp.zeros_like(acc)

    def couple(rank, k):
        if settle is not None:
            settle(k)

        def copy(i, carry):
            stage[i] = abuf[rank * pc + i]
            return carry

        lax.fori_loop(0, pc, copy, 0, unroll=4)

        def one(j, carry):
            t = g * quarter + j
            source = stage[slot_ref[t, rank]]
            x = x_ref[rank, j]
            h = jnp.dot(x, source, preferred_element_type=F32).astype(BF16)
            y = lax.dot_general(h, x, (((1,), (1,)), ((), ())), preferred_element_type=F32)
            acc[j] += fock_ref[t, rank] * y
            return carry

        lax.fori_loop(0, quarter, one, 0, unroll=4)

    couple(p, 0)

    def exchange(blocks):
        for k, rank in () if joined else blocks:
            across_wait(k, rank)
            mate_copy(k, rank, 3).start()

    def use(blocks):
        for k, rank in blocks:
            mate_wait(k, rank)
            couple(rank, k)

    landed, shared = [], []
    for step in range(1, steps + 1):
        for c in (1, 0, 2, 3)[:parts]:
            for d in (0, 1):
                rank = at(position + (-step if d == 0 else step), n)
                if c in parts_of(step, d):
                    arrive(step, d, c)
                    if step < steps and c in parts_of(step + 1, d):
                        ring_copy(step + 1, d, c).start()
                    k = 2 * step - 1 + (d if step < steps else 0)
                    if c == 1 and not joined:
                        across_copy(k, rank).start()
                    mate_copy(k, rank, c).start()
        exchange(landed)
        use(shared)
        shared = landed
        landed = [
            (2 * step - 1 + d, at(position + (-step if d == 0 else step), n))
            for d in ((0, 1) if step < steps else (0,))
        ]
    exchange(landed)
    use(shared)
    use(landed)

    def scaled(j):
        t = g * quarter + j
        row = jnp.broadcast_to(e_ref[pl.ds(t, 1), :], (width, width))
        return (-(k_ref[t] + acc[j]) / (row.T + row + fock_ref[t, n])).astype(BF16)

    if first:
        def result(j, carry):
            out_ref[j] = scaled(j)
            return carry

        lax.fori_loop(0, quarter, result, 0, unroll=2)
    else:
        def block(ref, group):
            return ref.at[pl.ds(group * quarter, quarter)]

        def result(j, carry):
            value = scaled(j)
            mine[j] = value
            out_ref[g * quarter + j] = value
            return carry

        lax.fori_loop(0, quarter, result, 0, unroll=2)
        over = remote(mine, block(out_ref, g), fs.at[0], fr.at[0], (p, across))
        beside = remote(mine, block(out_ref, g), fs.at[1], fr.at[1], (p, mate))
        corner = remote(
            block(out_ref, across), block(out_ref, across), fs.at[2], fr.at[2], (p, mate)
        )
        over.start()
        beside.start()
        remote(mine, block(out_ref, across), fs.at[0], fr.at[0], (p, across)).wait_recv()
        corner.start()
        remote(mine, block(out_ref, mate), fs.at[1], fr.at[1], (p, mate)).wait_recv()
        remote(mine, block(out_ref, diagonal), fs.at[2], fr.at[2], (p, mate)).wait_recv()
        over.wait_send()
        beside.wait_send()
        corner.wait_send()
        across_copy(0, p, 0, own_half(0)).wait_send()
        across_copy(0, p, 1, own_half(1)).wait_send()
        for c in range(4):
            mate_copy(0, p, c).wait_send()
    for k in range(1, n):
        if not joined:
            across_copy(k, p).wait_send()
        for c in range(4):
            mate_copy(k, p, c).wait_send()
    for step in range(1, steps + 1):
        for d in (0, 1):
            for c in parts_of(step, d):
                ring_copy(step, d, c).wait_send()


def intersections_alone(*args):
    steps = intersections(*args)
    next(steps)
    settle = next(steps)
    for k in range(args[0]):
        settle(k)
    next(steps, None)


def iteration_alone(n, first, *args):
    steps = iteration(n, first, False, True, *args)
    next(steps)
    try:
        steps.send(None)
    except StopIteration:
        pass


def opening(
    n, made, slot_ref, fock_ref, c_ref, dom_ref, start_ref, k_ref, e_ref, out_ref,
    x_ref, amp_ref, *scratch
):
    used = made + (len(scratch) - made) // 2
    blocks = intersections(n, slot_ref, c_ref, dom_ref, x_ref, *scratch[:made])
    next(blocks)
    amps = iteration(
        n, True, True, False, slot_ref, fock_ref, start_ref, x_ref, k_ref, e_ref, amp_ref,
        *scratch[made:used],
    )
    next(amps)
    settle = next(blocks)
    try:
        amps.send(settle)
    except StopIteration:
        pass
    amps = iteration(
        n, False, False, False, slot_ref, fock_ref, amp_ref, x_ref, k_ref, e_ref, out_ref,
        *scratch[used:],
    )
    next(amps)
    try:
        amps.send(None)
    except StopIteration:
        pass
    next(blocks, None)


def on_device(
    coefficients, domain, coupling_owner, coupling_slot, coupling_fock,
    exchange_integrals, pno_energy, pair_shift, amplitudes_start,
):
    n = lax.axis_size("pairs")
    pc, rows, width = coefficients.shape
    quarter = pc // lax.axis_size("grp")
    steps = n // 2
    named = coupling_owner[:, :, None] == jnp.arange(n, dtype=jnp.int32)[None, None, :]
    slots = jnp.sum(jnp.where(named, coupling_slot[:, :, None], 0), axis=1)
    focks = jnp.sum(jnp.where(named, coupling_fock[:, :, None], 0.0), axis=1)
    focks = jnp.concatenate([focks, pair_shift[:, None]], axis=1)
    vmem, smem = pl.BlockSpec(memory_space=pltpu.VMEM), pl.BlockSpec(memory_space=pltpu.SMEM)
    dma = pltpu.SemaphoreType.DMA

    def params(collective):
        return pltpu.CompilerParams(
            collective_id=collective, has_side_effects=True, vmem_limit_bytes=60 * 2**20
        )

    big = (width, width)
    x_shape = jax.ShapeDtypeStruct((n, quarter, *big), BF16)
    block_scratch = [
        pltpu.VMEM((n, pc, rows, width), BF16),
        pltpu.VMEM((n, pc, rows), jnp.int32),
        pltpu.VMEM((pc, width, NB), BF16),
        pltpu.VMEM((pc, NB, width), BF16),
        pltpu.VMEM((2, 2 * quarter, *big), F32),
        pltpu.VMEM((2, 2 * quarter, *big), F32),
        pltpu.VMEM((n, 2 * quarter, *big), F32),
        pltpu.VMEM((2, quarter, *big), F32),
        pltpu.VMEM((n, quarter, *big), F32),
        pltpu.VMEM((n, quarter, *big), F32),
        dma((2, steps, 3)), dma((2, steps, 3)),
        dma((n,)), dma((n,)), dma((n,)), dma((n,)),
    ]
    amp_scratch = [
        pltpu.VMEM((n * pc, *big), BF16),
        pltpu.VMEM((pc, *big), BF16),
        pltpu.VMEM((quarter, *big), F32),
        pltpu.VMEM((quarter, *big), BF16),
        dma((2, steps, 4)), dma((2, steps, 4)),
        dma((n, 4)), dma((n, 4)), dma((n + 1,)), dma((n + 1,)), dma((3,)), dma((3,)),
    ]
    half_shape = jax.ShapeDtypeStruct((quarter, *big), BF16)

    def iterate(first, start, x):
        return pl.pallas_call(
            functools.partial(iteration_alone, n, first),
            out_shape=half_shape if first else jax.ShapeDtypeStruct((pc, *big), BF16),
            in_specs=[smem, smem, vmem, vmem, vmem, vmem],
            out_specs=vmem,
            scratch_shapes=amp_scratch,
            compiler_params=params(1 if first else 2),
            name="first" if first else "second",
        )(slots, focks, start, x, exchange_integrals, pno_energy)

    held = n * width * (2 * pc * (rows + width) + 4 * width * 4 * quarter + 2 * width * quarter)
    if held < 40 * 2**20:
        return pl.pallas_call(
            functools.partial(opening, n, len(block_scratch)),
            out_shape=jax.ShapeDtypeStruct((pc, *big), BF16),
            in_specs=[smem, smem, vmem, vmem, vmem, vmem, vmem],
            out_specs=vmem,
            scratch_shapes=[
                pltpu.VMEM(x_shape.shape, BF16), pltpu.VMEM(half_shape.shape, BF16),
                *block_scratch, *amp_scratch, *amp_scratch,
            ],
            compiler_params=params(0),
            name="amplitudes",
        )(slots, focks, coefficients, domain, amplitudes_start, exchange_integrals, pno_energy).astype(F32)
    else:
        x = pl.pallas_call(
            functools.partial(intersections_alone, n),
            out_shape=x_shape,
            in_specs=[smem, vmem, vmem],
            out_specs=vmem,
            scratch_shapes=block_scratch,
            compiler_params=params(0),
            name="intersections",
        )(slots, coefficients, domain)
        amps = iterate(True, amplitudes_start, x)
    return iterate(False, amps, x).astype(F32)


def solution(mesh):
    placed = (
        P("pairs", "grp", None),
        P("pairs", "grp"),
        P("pairs", None),
        P("pairs", None),
        P("pairs", None),
        P("pairs", None, None),
        P("pairs", None),
        P("pairs"),
        P("pairs", None, None),
    )
    return jax.shard_map(
        on_device, mesh=mesh, in_specs=placed, out_specs=P("pairs", None, None), check_vma=False
    )
```
